256 devices in a mesh: front: 8 (over z), row: 32 (over x, y, core).
Axes of the slice: x: 4, y: 4, z: 8, core: 2. Of those that a mesh axis runs over, the one named last changes fastest.
Arguments:
- panels: bfloat16 [8, 4096, 1280], P('front', 'row'), may hold values from -6 to 6
- reflectors: bfloat16 [8, 4096, 512], P('front', 'row'), may hold values from -6 to 6
- block_coeffs: bfloat16 [8, 512, 512], P('front')
- block_mask: int32 [8, 32, 4], P('front', 'row'), may hold values 0 or 1
- block_starts: int32 [8, 4], P('front'), may hold values from 0 to 2048, as said below
- carry_map: int32 [8, 1024], P('front'), may hold values from 0 to 4095, as said below
Outputs:
- panels_out: bfloat16 [8, 4096, 1280], P('front', 'row')
The draws below stay inside these ranges and needn't reach their ends.
Inputs may be any that keep to these rules, and one draw needn't show every extreme that they name: `block_starts`: nondecreasing along the reflector blocks of a front. `carry_map`: within a front the targets are distinct, and carried row i lands in the 128-row block number i % 32, which receives exactly 32 carried rows, its last row among them.
All inputs are finite; a program needn't handle non-finite values. No bound on the sum of `block_mask` on one device may be relied on, other than what follows from the above.
Results may differ from the reference program's by a relative error of at most 0.017.
Values may be sent and summed in bfloat16 or wider, within the bound.
No kernel may reach another device: no remote copies, remote signals or barrier semaphores. Data moves between devices by JAX's collectives and lax.ppermute only.
A program may use at most 64 MiB of HBM per device.

```python
import jax
import jax.numpy as jnp

K = 512
RDEV = 128
NC = 1280
ROWS = 4096
FRONTS = 8


def draw_block_coeffs(key, part):
    first_key, second_key = jax.random.split(jax.random.fold_in(key, 7))
    scale_off = 1.0 / (K / 2.0 * (ROWS / 4.0) ** 0.5)
    diagonal = jax.random.uniform(first_key, (FRONTS, K), jnp.float32, 1.0, 2.0) / (ROWS / 4.0)
    offdiag = jax.random.normal(second_key, (FRONTS, K, K), jnp.float32) * scale_off
    upper = jnp.triu(offdiag, 1) + diagonal[:, :, None] * jnp.eye(K, dtype=jnp.float32)[None]
    return upper.astype(jnp.bfloat16)


def draw_block_starts(key, part):
    blocks = K // 128
    raw_starts = jax.random.randint(jax.random.fold_in(key, 11), (FRONTS, blocks), 0, ROWS // 2 + 1)
    sorted_starts = jnp.sort(raw_starts, axis=1)
    columns = jnp.arange(blocks)[None, :]
    fronts_idx = jnp.arange(FRONTS)[:, None]
    sorted_starts = jnp.where((columns == 0) & (fronts_idx == 0), 0, sorted_starts)
    sorted_starts = jnp.where((columns == blocks - 1) & (fronts_idx == FRONTS - 1), ROWS // 2, sorted_starts)
    return sorted_starts.astype(jnp.int32)


def draw_carry_map(key, part):
    row_count = ROWS // RDEV
    per_block = RDEV // 4
    subkeys = jax.random.split(jax.random.fold_in(key, 13), FRONTS * row_count)

    def pick_rows(subkey):
        others = jax.random.permutation(subkey, RDEV - 1)[:per_block - 1].astype(jnp.int32)
        return jnp.concatenate([others, jnp.full((1,), RDEV - 1, jnp.int32)])
    chosen = jax.vmap(pick_rows)(subkeys)
    chosen = chosen.reshape(FRONTS, row_count, per_block).astype(jnp.int32)
    offsets = (jnp.arange(row_count, dtype=jnp.int32) * RDEV)[None, :, None]
    targets = jnp.transpose(chosen + offsets, (0, 2, 1))
    return targets.reshape(FRONTS, per_block * row_count).astype(jnp.int32)


def place_ends(array, key, low, high):
    longest = array.shape.index(max(array.shape))
    spots = []
    for shift in (0, 1):
        where = [jax.random.randint(jax.random.fold_in(key, axis), (), 0, length) for axis, length in enumerate(array.shape)]
        where[longest] = (where[longest] + shift) % array.shape[longest]
        spots.append(tuple(where))
    return array.at[spots[0]].set(low).at[spots[1]].set(high)


def level_of(key, dims, shards, low, top_value):
    loudness, own = 1.0, jax.random.fold_in(key, 6)
    for axis_at, shards_of in shards:
        draws = jnp.exp(jax.random.uniform(jax.random.fold_in(own, axis_at), (shards_of,), jnp.float32, low / len(shards), top_value / len(shards)))
        loudness = loudness * jnp.repeat(draws, dims[axis_at] // shards_of).reshape([-1 if axis == axis_at else 1 for axis in range(len(dims))])
    return loudness


def bell_draw(key, extent, scale, most, cuts=(), kind=jnp.bfloat16):
    array = scale * jax.random.normal(key, extent, jnp.float32)
    if cuts:
        array = array * level_of(key, extent, cuts, -0.22, 0.18)
    return jnp.clip(array, -most, most).astype(kind)


def setup_inputs(seed: int = 0) -> dict:
    arg_keys = jax.random.split(jax.random.key(seed), 7)
    return {
        "panels": bell_draw(arg_keys[0], (FRONTS, ROWS, NC), 1.0, 6.0, ((0, 8), (1, 32))),
        "reflectors": bell_draw(arg_keys[1], (FRONTS, ROWS, K), 1.0, 6.0, ((0, 8), (1, 32))),
        "block_coeffs": draw_block_coeffs(jax.random.fold_in(arg_keys[6], 71), 0),
        "block_mask": place_ends((jax.random.randint(arg_keys[3], (FRONTS, ROWS // 128, K // 128), 0, 2) < 1).astype(jnp.int32), jax.random.fold_in(arg_keys[3], 1), 0, 1),
        "block_starts": draw_block_starts(jax.random.fold_in(arg_keys[6], 71), 0),
        "carry_map": draw_carry_map(jax.random.fold_in(arg_keys[6], 71), 0),
    }


def reference(panels, reflectors, block_coeffs, block_mask, block_starts, carry_map):
    row_ids = jnp.arange(ROWS, dtype=jnp.int32)
    results = []
    carried = None
    for front in range(FRONTS):
        mask_full = jnp.repeat(jnp.repeat(block_mask[front], 128, axis=0), 128, axis=1)
        start_cols = jnp.repeat(block_starts[front], 128)
        retained = (mask_full == 1) & (row_ids[:, None] >= start_cols[None, :])
        effective = jnp.where(retained, reflectors[front], jnp.zeros_like(reflectors[front]))
        assembled = panels[front].astype(jnp.float32)
        if front > 0:
            assembled = assembled.at[carry_map[front]].add(carried.astype(jnp.float32))
        assembled = assembled.astype(jnp.bfloat16)
        partial_value = jnp.dot(effective.T, assembled, preferred_element_type=jnp.float32)
        wcoef = partial_value.astype(jnp.bfloat16)
        mixed = jnp.dot(block_coeffs[front].T, wcoef, preferred_element_type=jnp.float32).astype(jnp.bfloat16)
        result = (assembled.astype(jnp.float32) - jnp.dot(effective, mixed, preferred_element_type=jnp.float32)).astype(jnp.bfloat16)
        results.append(result)
        carried = result[3 * ROWS // 4:]
    return jnp.stack(results)
```

```python
import jax
import jax.numpy as jnp
import numpy as np
from jax import lax
from jax.sharding import PartitionSpec as P

BF = jnp.bfloat16
F32 = jnp.float32


def mm(a, b, dims=((1,), (0,))):
    return lax.dot_general(a, b, (dims, ((), ())), preferred_element_type=F32)


def local(panels, reflectors, block_coeffs, block_mask, block_starts, carry_map):
    rows = lax.axis_size("row")
    fronts = lax.axis_size("front")
    row = lax.axis_index("row")
    front = lax.axis_index("front")
    span, cols = panels.shape[1:]
    width = reflectors.shape[2]
    part = cols // rows
    carried = carry_map.shape[1]
    each = carried // rows
    total = span * rows
    tail = total - carried

    ids = row * span + lax.broadcasted_iota(jnp.int32, (span, width), 0)
    starts = jnp.repeat(block_starts[0], 128)
    kept = (jnp.repeat(block_mask[0, 0], 128)[None, :] == 1) & (ids >= starts[None, :])
    own = jnp.where(kept, reflectors[0], jnp.zeros_like(reflectors[0]))
    eff = lax.all_gather(own, "row", axis=0, tiled=True)

    pieces = panels[0].T.reshape(rows, part, span)
    got = lax.all_to_all(pieces, "row", 0, 0, tiled=True)
    pan = got.transpose(1, 0, 2).reshape(part, total)

    targets = carry_map[0].reshape(each, rows).T
    offsets = targets - span * jnp.arange(rows, dtype=jnp.int32)[:, None]
    pick = (offsets[:, :, None] == jnp.arange(span, dtype=jnp.int32)).astype(BF)
    gath = lax.dot_general(
        pick, eff.reshape(rows, span, width), (((2,), (1,)), ((0,), (0,))), preferred_element_type=F32
    ).astype(BF).reshape(carried, width)
    low = eff[tail:].reshape(each, rows, width).transpose(1, 0, 2).reshape(carried, width)
    order = (jnp.arange(carried, dtype=jnp.int32) % each) * rows + jnp.arange(carried, dtype=jnp.int32) // each
    swap = (jnp.arange(carried, dtype=jnp.int32)[:, None] == order[None, :]).astype(BF)
    pan_low = mm(pan[:, tail:], swap).astype(BF)
    quarter = carried // 4
    inner = targets.reshape(-1)[carried - quarter:] - tail
    reach = (inner[:, None] == order[None, :]).astype(BF)

    coeffs = block_coeffs[0]
    base = mm(pan, eff)

    def mixed_of(cin):
        w = (base + mm(cin, gath)).astype(BF)
        return mm(w, coeffs).astype(BF)

    def advance(cin):
        m = mixed_of(cin)
        a = (pan_low.astype(F32) + mm(cin[:, carried - quarter:], reach)).astype(BF)
        return (a.astype(F32) - mm(m, low, ((1,), (1,)))).astype(BF)

    cin = jnp.zeros((part, carried), BF)
    for step in range(1, fronts):
        sent = advance(cin)
        came = lax.ppermute(sent, "front", [(step - 1, step)])
        cin = jnp.where(front == step, came, cin)

    m = mixed_of(cin)
    moved = lax.dot_general(
        cin.reshape(part, rows, each), pick, (((2,), (1,)), ((1,), (0,))), preferred_element_type=F32
    )
    a = (got.astype(F32) + moved).astype(BF)
    back = mm(m, eff, ((1,), (1,))).reshape(part, rows, span).transpose(1, 0, 2)
    out = (a.astype(F32) - back).astype(BF)
    home = lax.all_to_all(out, "row", 0, 0, tiled=True)
    return home.reshape(cols, span).T[None]


def solution(mesh):
    in_specs = (
        P("front", "row", None),
        P("front", "row", None),
        P("front", None, None),
        P("front", "row", None),
        P("front", None),
        P("front", None),
    )
    out_specs = P("front", "row", None)
    return jax.shard_map(local, mesh=mesh, in_specs=in_specs, out_specs=out_specs, check_vma=False)
```

```python
import functools

import jax
import jax.numpy as jnp
from jax import lax
from jax.experimental import pallas as pl
from jax.experimental.pallas import tpu as pltpu
from jax.sharding import PartitionSpec as P

BF = jnp.bfloat16
F32 = jnp.float32
SIDE = 4


def mm(a, b, dims=((1,), (0,))):
    return lax.dot_general(a, b, (dims, ((), ())), preferred_element_type=F32)


def place(x, y, core):
    return ((x % SIDE) * SIDE + y % SIDE) * 2 + core


def shift(second, step):
    pairs = []
    for x in range(SIDE):
        for y in range(SIDE):
            for core in range(2):
                along_x = (core == 0) != second
                pairs.append((place(x, y, core), place(x + step * along_x, y + step * (not along_x), core)))
    return pairs


SWAP = [(place(x, y, c), place(x, y, 1 - c)) for x in range(SIDE) for y in range(SIDE) for c in range(2)]


def assemble_kernel(row_ref, g0, g1, g2a, g2b, g3, s0, s1, s2a, s2b, s3, out_ref):
    row = row_ref[0]
    x, y, core = row // (2 * SIDE), (row // 2) % SIDE, row % 2
    for sibling, parts in enumerate((((g0, 0), (g1, 0), None, (g3, 0)), ((s0, 0), (s1, 0), None, (s3, 0)))):
        halves = (g2a, g2b) if sibling == 0 else (s2a, s2b)
        who = core if sibling == 0 else 1 - core
        for j in range(SIDE):
            for k in range(SIDE):
                dx = jnp.where(who == 0, k, j)
                dy = jnp.where(who == 0, j, k)
                block = (((x + dx) % SIDE) * SIDE + (y + dy) % SIDE) * 2 + who
                source = parts[j][0].at[k] if j != 2 else halves[k // 2].at[k % 2]
                out_ref[block] = source[...]


def gather_rows(own, row):
    pp = lambda value, pairs: lax.ppermute(value, "row", pairs)
    half = own.shape[0] // 2
    left = pp(own, shift(False, 1))
    right = pp(own, shift(False, -1))
    far_a = pp(left[:half], shift(False, 1))
    far_b = pp(right[half:], shift(False, -1))
    group = jnp.stack([own, right, jnp.concatenate([far_a, far_b]), left])
    left2 = pp(group, shift(True, 1))
    right2 = pp(group, shift(True, -1))
    far2_a = pp(left2[:2], shift(True, 1))
    far2_b = pp(right2[2:], shift(True, -1))
    mine = [group, right2, far2_a, far2_b, left2]
    theirs = [pp(value, SWAP) for value in mine]
    shape = jax.ShapeDtypeStruct((2 * SIDE * SIDE, *own.shape), own.dtype)
    vmem = pl.BlockSpec(memory_space=pltpu.VMEM)
    return pl.pallas_call(
        assemble_kernel,
        out_shape=shape,
        in_specs=[pl.BlockSpec(memory_space=pltpu.SMEM)] + [vmem] * 10,
        out_specs=vmem,
        compiler_params=pltpu.CompilerParams(vmem_limit_bytes=24 << 20),
        name="assemble",
    )(row.reshape(1), *mine, *theirs)


def local(panels, reflectors, block_coeffs, block_mask, block_starts, carry_map):
    rows = lax.axis_size("row")
    fronts = lax.axis_size("front")
    row = lax.axis_index("row")
    front = lax.axis_index("front")
    span, cols = panels.shape[1:]
    width = reflectors.shape[2]
    part = cols // rows
    carried = carry_map.shape[1]
    each = carried // rows
    total = span * rows
    tail = total - carried

    ids = row * span + lax.broadcasted_iota(jnp.int32, (span, width), 0)
    starts = jnp.repeat(block_starts[0], 128)
    kept = (jnp.repeat(block_mask[0, 0], 128)[None, :] == 1) & (ids >= starts[None, :])
    own = jnp.where(kept, reflectors[0], jnp.zeros_like(reflectors[0]))
    blocks = gather_rows(own, row)
    eff = blocks.reshape(total, width)

    pieces = panels[0].T.reshape(rows, part, span)
    got = lax.all_to_all(pieces, "row", 0, 0, tiled=True)
    pan = got.transpose(1, 0, 2).reshape(part, total)

    count = jnp.arange(carried, dtype=jnp.int32)
    targets = carry_map[0].reshape(each, rows).T
    offsets = targets - span * jnp.arange(rows, dtype=jnp.int32)[:, None]
    pick = (offsets[:, :, None] == jnp.arange(span, dtype=jnp.int32)).astype(BF)
    order = (count % each) * rows + count // each
    swap = (count[:, None] == order[None, :]).astype(BF)
    quarter = carried // 4
    inner = targets.reshape(-1)[carried - quarter :] - tail
    reach = (inner[:, None] == order[None, :]).astype(F32)

    coeffs = block_coeffs[0]
    pan_low = mm(pan[:, tail:], swap).astype(BF)
    low = eff[tail:].reshape(each, rows, width).transpose(1, 0, 2).reshape(carried, width)
    base = mm(mm(pan, eff).astype(BF), coeffs)
    first = pan_low.astype(F32) - mm(base.astype(BF), low, ((1,), (1,)))

    sent = first.astype(BF)
    came = lax.ppermute(sent, "front", [(0, 1)])
    cin = came

    gath = lax.dot_general(
        pick, blocks, (((2,), (1,)), ((0,), (0,))), preferred_element_type=F32
    ).astype(BF).reshape(carried, width)
    turn = mm(gath, coeffs).astype(BF)
    fall = mm(turn, low, ((1,), (1,)))
    hop = jnp.concatenate([-fall[: carried - quarter], reach - fall[carried - quarter :]]).astype(BF)

    for step in range(2, fronts):
        sent = (first + mm(came, hop)).astype(BF)
        came = lax.ppermute(sent, "front", [(step - 1, step)])
        cin = jnp.where(front == step, came, cin)

    m = (base + mm(cin, turn)).astype(BF)
    moved = lax.dot_general(
        cin.reshape(part, rows, each), pick, (((2,), (1,)), ((1,), (0,))), preferred_element_type=F32
    )
    a = (got.astype(F32) + moved).astype(BF)
    back = mm(m, eff, ((1,), (1,))).reshape(part, rows, span).transpose(1, 0, 2)
    out = (a.astype(F32) - back).astype(BF)
    home = lax.all_to_all(out, "row", 0, 0, tiled=True)
    return home.reshape(cols, span).T[None]


def solution(mesh):
    in_specs = (
        P("front", "row", None),
        P("front", "row", None),
        P("front", None, None),
        P("front", "row", None),
        P("front", None),
        P("front", None),
    )
    out_specs = P("front", "row", None)
    return jax.shard_map(local, mesh=mesh, in_specs=in_specs, out_specs=out_specs, check_vma=False)
```

```python
import jax
import jax.numpy as jnp
from jax import lax
from jax.experimental import pallas as pl
from jax.experimental.pallas import tpu as pltpu
from jax.sharding import PartitionSpec as P

BF = jnp.bfloat16
F32 = jnp.float32
I32 = jnp.int32
SIDE = 4
ROWS = 32
SPAN = 128
EACH = 32
CARRIED = ROWS * EACH
TAIL = 24
WIDTH = 512


def mm(a, b, dims=((1,), (0,))):
    return lax.dot_general(a, b, (dims, ((), ())), preferred_element_type=F32)


def place(x, y, core):
    return ((x % SIDE) * SIDE + y % SIDE) * 2 + core


def shift(second, step):
    pairs = []
    for x in range(SIDE):
        for y in range(SIDE):
            for core in range(2):
                along_x = (core == 0) != second
                pairs.append((place(x, y, core), place(x + step * along_x, y + step * (not along_x), core)))
    return pairs


SWAP = [(place(x, y, c), place(x, y, 1 - c)) for x in range(SIDE) for y in range(SIDE) for c in range(2)]

VMEM = pl.BlockSpec(memory_space=pltpu.VMEM)
SMEM = pl.BlockSpec(memory_space=pltpu.SMEM)


def call(kernel, outs, specs, name, limit=20, scratch=(), cost=None):
    return pl.pallas_call(
        kernel,
        out_shape=outs,
        in_specs=specs,
        out_specs=jax.tree.map(lambda _: VMEM, outs),
        scratch_shapes=scratch,
        compiler_params=pltpu.CompilerParams(vmem_limit_bytes=limit << 20),
        cost_estimate=cost,
        name=name,
    )


def shape(dims, dtype=BF):
    return jax.ShapeDtypeStruct(dims, dtype)


def mask_kernel(row, mask, starts, refl, own):
    ids = row[0] * SPAN + lax.broadcasted_iota(I32, (SPAN, 128), 0)
    for k in range(WIDTH // 128):
        kept = (ids >= starts[0, k]) & (mask[0, 0, k] == 1)
        part = refl[0, :, k * 128 : (k + 1) * 128].astype(F32)
        own[:, k * 128 : (k + 1) * 128] = jnp.where(kept, part, 0.0).astype(BF)


def turn_kernel(panels, out):
    for k in range(panels.shape[2] // 128):
        part = panels[0, :, k * 128 : (k + 1) * 128]
        out[k * 128 : (k + 1) * 128, :] = part.T


def slots(row, sibling):
    x, y, core = row // (2 * SIDE), (row // 2) % SIDE, row % 2
    who = 1 - core if sibling else core
    for j in range(SIDE):
        for k in range(SIDE):
            dx = jnp.where(who == 0, k, j)
            dy = jnp.where(who == 0, j, k)
            yield j, k, (((x + dx) % SIDE) * SIDE + (y + dy) % SIDE) * 2 + who


def base_kernel(row, g0, g1, g2a, g2b, g3, s0, s1, s2a, s2b, s3, got, coeffs, eff, base, first, sent):
    acc = jnp.zeros(base.shape, F32)
    for sibling, parts in enumerate(((g0, g1, g2a, g2b, g3), (s0, s1, s2a, s2b, s3))):
        held = None
        for j, k, block in slots(row[0], sibling):
            if j == 2:
                source = parts[2 + k // 2].at[k % 2]
            else:
                source = parts[j if j < 2 else 4].at[k]
            tile = source[...]
            eff[block] = tile
            if held is None:
                held = (got[block], tile)
            else:
                lhs = jnp.concatenate([held[0], got[block]], axis=1)
                acc += mm(lhs, jnp.concatenate([held[1], tile], axis=0))
                held = None
    m = mm(acc.astype(BF), coeffs[0])
    base[...] = m
    m = m.astype(BF)
    for t in range(TAIL, ROWS, 2):
        low = eff[t : t + 2].reshape(2 * SPAN, WIDTH)
        have = jnp.concatenate([got[t], got[t + 1]], axis=1).astype(F32)
        res = have - mm(m, low, ((1,), (1,)))
        at = pl.ds((t - TAIL) * SPAN, 2 * SPAN)
        first[:, at] = res
        sent[:, at] = res.astype(BF)


def hop_kernel(offsets, eff, coeffs, turn, hop, gath, fall):
    lane = lax.broadcasted_iota(I32, (2 * EACH, 2 * SPAN), 1)
    for b in range(0, ROWS, 2):
        where = jnp.concatenate([offsets[:, b : b + 1], offsets[:, b + 1 : b + 2] + SPAN], axis=0)
        pick = (where == lane).astype(F32).astype(BF)
        rows = mm(pick, eff[b : b + 2].reshape(2 * SPAN, WIDTH))
        for h in range(2):
            for k in range(WIDTH // 128):
                tile = rows[h * EACH : (h + 1) * EACH, k * 128 : (k + 1) * 128]
                gath[k, pl.ds(b + h, EACH, stride=ROWS), :] = tile
    for r in range(0, CARRIED, 256):
        wide = jnp.concatenate([gath[k, r : r + 256, :].astype(BF) for k in range(WIDTH // 128)], axis=1)
        turn[r : r + 256, :] = mm(wide, coeffs[0]).astype(BF)
    lane = lax.broadcasted_iota(I32, (EACH, SPAN), 1)
    for t in range(TAIL, ROWS, 2):
        low = eff[t : t + 2].reshape(2 * SPAN, WIDTH)
        for r in range(0, CARRIED, 256):
            down = -mm(turn[r : r + 256, :], low, ((1,), (1,)))
            for h in range(2):
                fall[h, r : r + 256, :] = down[:, h * SPAN : (h + 1) * SPAN]
        for h in range(2):
            pick = (offsets[:, t + h : t + h + 1] == lane).astype(F32)
            at = (h, pl.ds(t + h, EACH, stride=ROWS), slice(None))
            fall[at] = fall[at] + pick
            hop[:, (t + h - TAIL) * SPAN : (t + h - TAIL + 1) * SPAN] = fall[h].astype(BF)


def table_kernel(offsets, order, spread):
    for r in range(0, CARRIED, 128):
        down = r + lax.broadcasted_iota(I32, (128, CARRIED), 0)
        right = lax.broadcasted_iota(I32, (128, CARRIED), 1)
        order[r : r + 128, :] = ((right % EACH) * ROWS + right // EACH == down).astype(F32).astype(BF)
    lane = lax.broadcasted_iota(I32, (EACH, 8 * SPAN), 1)
    for b in range(ROWS):
        where = offsets[:, b : b + 1] + (b % 8) * SPAN
        spread[b * EACH : (b + 1) * EACH, :] = (where == lane).astype(F32).astype(BF)


def last_kernel(c1, c2, c3, c4, c5, c6, c7, base, turn, order, spread, got, eff, out):
    cin = c1[...].astype(F32)
    for c in (c2, c3, c4, c5, c6, c7):
        cin += c[...].astype(F32)
    cin = cin.astype(BF)
    m = (base[...] + mm(cin, turn[...])).astype(BF)
    sorted_in = mm(cin, order[...]).astype(BF)
    for g in range(4):
        moved = mm(sorted_in[:, g * 256 : (g + 1) * 256], spread[g * 256 : (g + 1) * 256, :])
        for p in range(0, 8, 2):
            b = 8 * g + p
            have = jnp.concatenate([got[b], got[b + 1]], axis=1).astype(F32)
            a = (have + moved[:, p * SPAN : (p + 2) * SPAN]).astype(BF).astype(F32)
            back = mm(m, eff[b : b + 2].reshape(2 * SPAN, WIDTH), ((1,), (1,)))
            res = (a - back).astype(BF)
            out[b] = res[:, :SPAN]
            out[b + 1] = res[:, SPAN:]


def gather_rows(own):
    pp = lambda value, pairs: lax.ppermute(value, "row", pairs)
    half = own.shape[0] // 2
    left = pp(own, shift(False, 1))
    right = pp(own, shift(False, -1))
    far_a = pp(left[:half], shift(False, 1))
    far_b = pp(right[half:], shift(False, -1))
    group = jnp.stack([own, right, jnp.concatenate([far_a, far_b]), left])
    left2 = pp(group, shift(True, 1))
    right2 = pp(group, shift(True, -1))
    far2_a = pp(left2[:2], shift(True, 1))
    far2_b = pp(right2[2:], shift(True, -1))
    mine = [group, right2, far2_a, far2_b, left2]
    theirs = [pp(value, SWAP) for value in mine]
    return mine + theirs


def local(panels, reflectors, block_coeffs, block_mask, block_starts, carry_map):
    fronts = lax.axis_size("front")
    row = lax.axis_index("row").reshape(1)
    cols = panels.shape[2]
    part = cols // ROWS

    pieces = call(turn_kernel, shape((cols, SPAN)), [VMEM], "flip")(panels)
    own = call(mask_kernel, shape((SPAN, WIDTH)), [SMEM] * 3 + [VMEM], "mask")(
        row, block_mask, block_starts, reflectors
    )
    got = lax.all_to_all(pieces.reshape(ROWS, part, SPAN), "row", 0, 0, tiled=True)
    parts = gather_rows(own)

    offsets = carry_map[0].reshape(EACH, ROWS) - SPAN * jnp.arange(ROWS, dtype=I32)
    order, spread = call(
        table_kernel, (shape((CARRIED, CARRIED)), shape((CARRIED, 8 * SPAN))), [VMEM], "tables"
    )(offsets)

    eff, base, first, sent = call(
        base_kernel,
        (
            shape((ROWS, SPAN, WIDTH)),
            shape((part, WIDTH), F32),
            shape((part, CARRIED), F32),
            shape((part, CARRIED)),
        ),
        [SMEM] + [VMEM] * 12,
        "base",
    )(row, *parts, got, block_coeffs)

    came = [lax.ppermute(sent, "front", [(0, 1)])]
    turn, hop = call(
        hop_kernel,
        (shape((CARRIED, WIDTH)), shape((CARRIED, CARRIED))),
        [VMEM] * 3,
        "hop",
        scratch=[pltpu.VMEM((WIDTH // 128, CARRIED, 128), F32), pltpu.VMEM((2, CARRIED, SPAN), F32)],
    )(offsets, eff, block_coeffs)
    for step in range(2, fronts):
        sent = (first + mm(came[-1], hop)).astype(BF)
        came.append(lax.ppermute(sent, "front", [(step - 1, step)]))

    none = [jnp.zeros_like(sent)] * (7 - len(came))
    out = call(last_kernel, shape((ROWS, part, SPAN)), [VMEM] * 13, "last")(
        *came, *none, base, turn, order, spread, got, eff
    )
    home = lax.all_to_all(out, "row", 0, 0, tiled=True)
    return home.reshape(cols, SPAN).T[None]


def solution(mesh):
    in_specs = (
        P("front", "row", None),
        P("front", "row", None),
        P("front", None, None),
        P("front", "row", None),
        P("front", None),
        P("front", None),
    )
    out_specs = P("front", "row", None)
    return jax.shard_map(local, mesh=mesh, in_specs=in_specs, out_specs=out_specs, check_vma=False)
```

```python
import jax
import jax.numpy as jnp
from jax import lax
from jax.experimental import pallas as pl
from jax.experimental.pallas import tpu as pltpu
from jax.sharding import PartitionSpec as P


BF = jnp.bfloat16
F32 = jnp.float32
I32 = jnp.int32
SIDE = 4
ROWS = 32
SPAN = 128
EACH = 32
CARRIED = ROWS * EACH
TAIL = 24
WIDTH = 512


def mm(a, b, dims=((1,), (0,))):
    return lax.dot_general(a, b, (dims, ((), ())), preferred_element_type=F32)


def place(x, y, core):
    return ((x % SIDE) * SIDE + y % SIDE) * 2 + core


def shift(second, step):
    pairs = []
    for x in range(SIDE):
        for y in range(SIDE):
            for core in range(2):
                along_x = (core == 0) != second
                pairs.append((place(x, y, core), place(x + step * along_x, y + step * (not along_x), core)))
    return pairs


SWAP = [(place(x, y, c), place(x, y, 1 - c)) for x in range(SIDE) for y in range(SIDE) for c in range(2)]

VMEM = pl.BlockSpec(memory_space=pltpu.VMEM)
SMEM = pl.BlockSpec(memory_space=pltpu.SMEM)
HBM = pl.BlockSpec(memory_space=pltpu.HBM)


def call(kernel, outs, specs, limit=20, scratch=(), cost=None):
    return pl.pallas_call(
        kernel,
        out_shape=outs,
        in_specs=specs,
        out_specs=jax.tree.map(lambda _: VMEM, outs),
        scratch_shapes=scratch,
        compiler_params=pltpu.CompilerParams(vmem_limit_bytes=limit << 20),
        cost_estimate=cost,
    )


def shape(dims, dtype=BF):
    return jax.ShapeDtypeStruct(dims, dtype)


def mask_kernel(row, mask, starts, refl, own, mask_s, starts_s, refl_v, sems):
    moves = [
        pltpu.make_async_copy(source, target, sems.at[i])
        for i, (source, target) in enumerate(((refl, refl_v), (mask, mask_s), (starts, starts_s)))
    ]
    for move in moves:
        move.start()
    for move in moves:
        move.wait()
    ids = row[0] * SPAN + lax.broadcasted_iota(I32, (SPAN, 128), 0)
    for k in range(WIDTH // 128):
        kept = (ids >= starts_s[0, k]) & (mask_s[0, 0, k] == 1)
        part = refl_v[0, :, k * 128 : (k + 1) * 128].astype(F32)
        own[:, k * 128 : (k + 1) * 128] = jnp.where(kept, part, 0.0).astype(BF)


def turn_kernel(panels, out):
    for k in range(panels.shape[2] // 128):
        part = panels[0, :, k * 128 : (k + 1) * 128]
        out[k * 128 : (k + 1) * 128, :] = part.T


def slots(row, sibling):
    x, y, core = row // (2 * SIDE), (row // 2) % SIDE, row % 2
    who = 1 - core if sibling else core
    for j in range(SIDE):
        for k in range(SIDE):
            dx = jnp.where(who == 0, k, j)
            dy = jnp.where(who == 0, j, k)
            yield j, k, (((x + dx) % SIDE) * SIDE + (y + dy) % SIDE) * 2 + who


def base_kernel(row, *refs):
    mine, theirs, (got, coeffs, eff, base, first, sent) = refs[:8], refs[8:16], refs[16:]
    acc = jnp.zeros(base.shape, F32)
    for sibling, parts in enumerate((mine, theirs)):
        held = None
        for j, k, block in slots(row[0], sibling):
            tile = parts[2 * j + k // 2][k % 2]
            eff[block] = tile
            if held is None:
                held = (got[block], tile)
            else:
                lhs = jnp.concatenate([held[0], got[block]], axis=1)
                acc += mm(lhs, jnp.concatenate([held[1], tile], axis=0))
                held = None
    m = mm(acc.astype(BF), coeffs[0])
    base[...] = m
    m = m.astype(BF)
    for t in range(TAIL, ROWS, 2):
        low = eff[t : t + 2].reshape(2 * SPAN, WIDTH)
        have = jnp.concatenate([got[t], got[t + 1]], axis=1).astype(F32)
        res = have - mm(m, low, ((1,), (1,)))
        at = pl.ds((t - TAIL) * SPAN, 2 * SPAN)
        first[:, at] = res
        sent[:, at] = res.astype(BF)


def hop_kernel(offsets, eff, coeffs, turn, hop, gath, fall):
    lane = lax.broadcasted_iota(I32, (2 * EACH, 2 * SPAN), 1)
    for b in range(0, ROWS, 2):
        where = jnp.concatenate([offsets[:, b : b + 1], offsets[:, b + 1 : b + 2] + SPAN], axis=0)
        pick = (where == lane).astype(F32).astype(BF)
        rows = mm(pick, eff[b : b + 2].reshape(2 * SPAN, WIDTH))
        for h in range(2):
            for k in range(WIDTH // 128):
                tile = rows[h * EACH : (h + 1) * EACH, k * 128 : (k + 1) * 128]
                gath[k, pl.ds(b + h, EACH, stride=ROWS), :] = tile
    for r in range(0, CARRIED, 256):
        wide = jnp.concatenate([gath[k, r : r + 256, :].astype(BF) for k in range(WIDTH // 128)], axis=1)
        turn[r : r + 256, :] = mm(wide, coeffs[0]).astype(BF)
    lane = lax.broadcasted_iota(I32, (EACH, SPAN), 1)
    for t in range(TAIL, ROWS, 2):
        low = eff[t : t + 2].reshape(2 * SPAN, WIDTH)
        for r in range(0, CARRIED, 256):
            down = -mm(turn[r : r + 256, :], low, ((1,), (1,)))
            for h in range(2):
                fall[h, r : r + 256, :] = down[:, h * SPAN : (h + 1) * SPAN]
        for h in range(2):
            pick = (offsets[:, t + h : t + h + 1] == lane).astype(F32)
            at = (h, pl.ds(t + h, EACH, stride=ROWS), slice(None))
            fall[at] = fall[at] + pick
            hop[:, (t + h - TAIL) * SPAN : (t + h - TAIL + 1) * SPAN] = fall[h].astype(BF)


def table_kernel(offsets, order, spread):
    for r in range(0, CARRIED, 128):
        down = r + lax.broadcasted_iota(I32, (128, CARRIED), 0)
        right = lax.broadcasted_iota(I32, (128, CARRIED), 1)
        order[r : r + 128, :] = ((right % EACH) * ROWS + right // EACH == down).astype(F32).astype(BF)
    lane = lax.broadcasted_iota(I32, (EACH, 8 * SPAN), 1)
    for b in range(ROWS):
        where = offsets[:, b : b + 1] + (b % 8) * SPAN
        spread[b * EACH : (b + 1) * EACH, :] = (where == lane).astype(F32).astype(BF)


def last_kernel(c1, c2, c3, c4, c5, c6, c7, base, turn, order, spread, got, eff, out):
    cin = c1[...].astype(F32)
    for c in (c2, c3, c4, c5, c6, c7):
        cin += c[...].astype(F32)
    cin = cin.astype(BF)
    m = (base[...] + mm(cin, turn[...])).astype(BF)
    sorted_in = mm(cin, order[...]).astype(BF)
    for g in range(4):
        moved = mm(sorted_in[:, g * 256 : (g + 1) * 256], spread[g * 256 : (g + 1) * 256, :])
        for p in range(0, 8, 2):
            b = 8 * g + p
            have = jnp.concatenate([got[b], got[b + 1]], axis=1).astype(F32)
            a = (have + moved[:, p * SPAN : (p + 2) * SPAN]).astype(BF).astype(F32)
            back = mm(m, eff[b : b + 2].reshape(2 * SPAN, WIDTH), ((1,), (1,)))
            res = (a - back).astype(BF)
            out[b] = res[:, :SPAN]
            out[b + 1] = res[:, SPAN:]


def gather_rows(own):
    pp = lambda value, pairs: lax.ppermute(value, "row", pairs)
    half = own.shape[0] // 2
    right = pp(own, shift(False, -1))
    left = pp(own, shift(False, 1))
    far_a = pp(left[:half], shift(False, 1))
    far_b = pp(right[half:], shift(False, -1))
    near = jnp.stack([own, right])
    near_left = pp(near, shift(True, 1))
    near_right = pp(near, shift(True, -1))
    rest = jnp.stack([jnp.concatenate([far_a, far_b]), left])
    rest_right = pp(rest, shift(True, -1))
    rest_left = pp(rest, shift(True, 1))
    near_far = pp(near_left, shift(True, 1))
    rest_far = pp(rest_right, shift(True, -1))
    mine = [near, rest, near_right, rest_right, near_far, rest_far, near_left, rest_left]
    theirs = [pp(value, SWAP) for value in mine]
    return mine + theirs


def work(panels, reflectors, block_coeffs, block_mask, block_starts, carry_map):
    fronts = lax.axis_size("front")
    row = lax.axis_index("row").reshape(1)
    cols = panels.shape[2]
    part = cols // ROWS

    pieces = call(turn_kernel, shape((cols, SPAN)), [VMEM])(panels)
    own = call(
        mask_kernel,
        shape((SPAN, WIDTH)),
        [SMEM] + [HBM] * 3,
        scratch=[
            pltpu.SMEM(block_mask.shape, I32),
            pltpu.SMEM(block_starts.shape, I32),
            pltpu.VMEM(reflectors.shape, BF),
            pltpu.SemaphoreType.DMA((3,)),
        ],
    )(row, block_mask, block_starts, reflectors)
    got = lax.all_to_all(pieces.reshape(ROWS, part, SPAN), "row", 0, 0, tiled=True)
    parts = gather_rows(own)

    offsets = carry_map[0].reshape(EACH, ROWS) - SPAN * jnp.arange(ROWS, dtype=I32)
    order, spread = call(table_kernel, (shape((CARRIED, CARRIED)), shape((CARRIED, 8 * SPAN))), [VMEM])(offsets)

    eff, base, first, sent = call(
        base_kernel,
        (
            shape((ROWS, SPAN, WIDTH)),
            shape((part, WIDTH), F32),
            shape((part, CARRIED), F32),
            shape((part, CARRIED)),
        ),
        [SMEM] + [VMEM] * 18,
    )(row, *parts, got, block_coeffs)

    came = [lax.ppermute(sent, "front", [(0, 1)])]
    turn, hop = call(
        hop_kernel,
        (shape((CARRIED, WIDTH)), shape((CARRIED, CARRIED))),
        [VMEM] * 3,
        scratch=[pltpu.VMEM((WIDTH // 128, CARRIED, 128), F32), pltpu.VMEM((2, CARRIED, SPAN), F32)],
    )(offsets, eff, block_coeffs)
    for step in range(2, fronts):
        sent = (first + mm(came[-1], hop)).astype(BF)
        came.append(lax.ppermute(sent, "front", [(step - 1, step)]))

    none = [jnp.zeros_like(sent)] * (7 - len(came))
    out = call(last_kernel, shape((ROWS, part, SPAN)), [VMEM] * 13)(*came, *none, base, turn, order, spread, got, eff)
    home = lax.all_to_all(out, "row", 0, 0, tiled=True)
    return home.reshape(cols, SPAN).T[None]


def solution(mesh):
    in_specs = (
        P("front", "row", None),
        P("front", "row", None),
        P("front", None, None),
        P("front", "row", None),
        P("front", None),
        P("front", None),
    )
    out_specs = P("front", "row", None)
    return jax.shard_map(work, mesh=mesh, in_specs=in_specs, out_specs=out_specs, check_vma=False)
```

```python
import jax
import jax.numpy as jnp
from jax import lax
from jax.experimental import pallas as pl
from jax.experimental.pallas import tpu as pltpu
from jax.sharding import PartitionSpec as P


BF = jnp.bfloat16
F32 = jnp.float32
I32 = jnp.int32
SIDE = 4
ROWS = 32
SPAN = 128
EACH = 32
CARRIED = ROWS * EACH
TAIL = 24
WIDTH = 512


def mm(a, b, dims=((1,), (0,))):
    return lax.dot_general(a, b, (dims, ((), ())), preferred_element_type=F32)


def place(x, y, core):
    return ((x % SIDE) * SIDE + y % SIDE) * 2 + core


def moves(second, step):
    pairs = []
    for x in range(SIDE):
        for y in range(SIDE):
            for core in range(2):
                along_x = (core == 0) != second
                to_x, to_y = (step(x), y) if along_x else (x, step(y))
                pairs.append((place(x, y, core), place(to_x, to_y, core)))
    return pairs


def near_mate(p):
    return p ^ 1


def far_mate(p):
    return p + 1 if p % 2 else p - 1


SWAP = [(place(x, y, c), place(x, y, 1 - c)) for x in range(SIDE) for y in range(SIDE) for c in range(2)]

VMEM = pl.BlockSpec(memory_space=pltpu.VMEM)
SMEM = pl.BlockSpec(memory_space=pltpu.SMEM)
HBM = pl.BlockSpec(memory_space=pltpu.HBM)


def call(kernel, outs, specs, limit=20, scratch=(), cost=None):
    return pl.pallas_call(
        kernel,
        out_shape=outs,
        in_specs=specs,
        out_specs=jax.tree.map(lambda _: VMEM, outs),
        scratch_shapes=scratch,
        compiler_params=pltpu.CompilerParams(vmem_limit_bytes=limit << 20),
        cost_estimate=cost,
    )


def shape(dims, dtype=BF):
    return jax.ShapeDtypeStruct(dims, dtype)


def mask_kernel(row, mask, starts, refl, own, mask_s, starts_s, refl_v, sems):
    moves = [
        pltpu.make_async_copy(source, target, sems.at[i])
        for i, (source, target) in enumerate(((refl, refl_v), (mask, mask_s), (starts, starts_s)))
    ]
    for move in moves:
        move.start()
    for move in moves:
        move.wait()
    ids = row[0] * SPAN + lax.broadcasted_iota(I32, (SPAN, 128), 0)
    for k in range(WIDTH // 128):
        kept = (ids >= starts_s[0, k]) & (mask_s[0, 0, k] == 1)
        part = refl_v[0, :, k * 128 : (k + 1) * 128].astype(F32)
        own[:, k * 128 : (k + 1) * 128] = jnp.where(kept, part, 0.0).astype(BF)


def turn_kernel(panels, out):
    for k in range(panels.shape[2] // 128):
        part = panels[0, :, k * 128 : (k + 1) * 128]
        out[k * 128 : (k + 1) * 128, :] = part.T


def slots(row, sibling):
    x, y, core = row // (2 * SIDE), (row // 2) % SIDE, row % 2
    who = 1 - core if sibling else core
    one, two = jnp.where(who == 0, x, y), jnp.where(who == 0, y, x)
    near = one + 1 - 2 * (one % 2)
    far = (one + SIDE - 1 + 2 * (one % 2)) % SIDE
    beyond = far + 1 - 2 * (far % 2)
    for j in range(SIDE):
        for k, held in enumerate((one, near, far, beyond)):
            other = (two + j) % SIDE
            at_x, at_y = jnp.where(who == 0, held, other), jnp.where(who == 0, other, held)
            yield j, k, (at_x * SIDE + at_y) * 2 + who


def base_kernel(row, *refs):
    mine, theirs, (got, coeffs, eff, base, first, sent) = refs[:8], refs[8:16], refs[16:]
    acc = jnp.zeros(base.shape, F32)
    for sibling, parts in enumerate((mine, theirs)):
        held = None
        for j, k, block in slots(row[0], sibling):
            tile = parts[2 * j + k // 2][k % 2]
            eff[block] = tile
            if held is None:
                held = (got[block], tile)
            else:
                lhs = jnp.concatenate([held[0], got[block]], axis=1)
                acc += mm(lhs, jnp.concatenate([held[1], tile], axis=0))
                held = None
    m = mm(acc.astype(BF), coeffs[0])
    base[...] = m
    m = m.astype(BF)
    for t in range(TAIL, ROWS, 2):
        low = eff[t : t + 2].reshape(2 * SPAN, WIDTH)
        have = jnp.concatenate([got[t], got[t + 1]], axis=1).astype(F32)
        res = have - mm(m, low, ((1,), (1,)))
        at = pl.ds((t - TAIL) * SPAN, 2 * SPAN)
        first[:, at] = res
        sent[:, at] = res.astype(BF)


def unfold(carry):
    rows = jnp.concatenate([carry[:, j * ROWS : (j + 1) * ROWS] for j in range(EACH)], axis=0)
    return rows - SPAN * lax.broadcasted_iota(I32, (EACH, ROWS), 1)


def hop_kernel(carry, eff, coeffs, turn, hop, gath, fall):
    offsets = unfold(carry[...])
    lane = lax.broadcasted_iota(I32, (2 * EACH, 2 * SPAN), 1)
    for b in range(0, ROWS, 2):
        where = jnp.concatenate([offsets[:, b : b + 1], offsets[:, b + 1 : b + 2] + SPAN], axis=0)
        pick = (where == lane).astype(F32).astype(BF)
        rows = mm(pick, eff[b : b + 2].reshape(2 * SPAN, WIDTH))
        for h in range(2):
            for k in range(WIDTH // 128):
                tile = rows[h * EACH : (h + 1) * EACH, k * 128 : (k + 1) * 128]
                gath[k, pl.ds(b + h, EACH, stride=ROWS), :] = tile
    for r in range(0, CARRIED, 256):
        wide = jnp.concatenate([gath[k, r : r + 256, :].astype(BF) for k in range(WIDTH // 128)], axis=1)
        turn[r : r + 256, :] = mm(wide, coeffs[0]).astype(BF)
    lane = lax.broadcasted_iota(I32, (EACH, SPAN), 1)
    for t in range(TAIL, ROWS, 2):
        low = eff[t : t + 2].reshape(2 * SPAN, WIDTH)
        for r in range(0, CARRIED, 256):
            down = -mm(turn[r : r + 256, :], low, ((1,), (1,)))
            for h in range(2):
                fall[h, r : r + 256, :] = down[:, h * SPAN : (h + 1) * SPAN]
        for h in range(2):
            pick = (offsets[:, t + h : t + h + 1] == lane).astype(F32)
            at = (h, pl.ds(t + h, EACH, stride=ROWS), slice(None))
            fall[at] = fall[at] + pick
            hop[:, (t + h - TAIL) * SPAN : (t + h - TAIL + 1) * SPAN] = fall[h].astype(BF)


def table_kernel(carry, order, spread):
    offsets = unfold(carry[...])
    for r in range(0, CARRIED, 128):
        down = r + lax.broadcasted_iota(I32, (128, CARRIED), 0)
        right = lax.broadcasted_iota(I32, (128, CARRIED), 1)
        order[r : r + 128, :] = ((right % EACH) * ROWS + right // EACH == down).astype(F32).astype(BF)
    lane = lax.broadcasted_iota(I32, (EACH, 8 * SPAN), 1)
    for b in range(ROWS):
        where = offsets[:, b : b + 1] + (b % 8) * SPAN
        spread[b * EACH : (b + 1) * EACH, :] = (where == lane).astype(F32).astype(BF)


def last_kernel(c1, c2, c3, c4, c5, c6, c7, base, turn, order, spread, got, eff, out):
    cin = c1[...].astype(F32)
    for c in (c2, c3, c4, c5, c6, c7):
        cin += c[...].astype(F32)
    cin = cin.astype(BF)
    m = (base[...] + mm(cin, turn[...])).astype(BF)
    sorted_in = mm(cin, order[...]).astype(BF)
    for g in range(4):
        moved = mm(sorted_in[:, g * 256 : (g + 1) * 256], spread[g * 256 : (g + 1) * 256, :])
        for p in range(0, 8, 2):
            b = 8 * g + p
            have = jnp.concatenate([got[b], got[b + 1]], axis=1).astype(F32)
            a = (have + moved[:, p * SPAN : (p + 2) * SPAN]).astype(BF).astype(F32)
            back = mm(m, eff[b : b + 2].reshape(2 * SPAN, WIDTH), ((1,), (1,)))
            res = (a - back).astype(BF)
            out[b] = res[:, :SPAN]
            out[b + 1] = res[:, SPAN:]


def gather_rows(own):
    pp = lambda value, pairs: lax.ppermute(value, "row", pairs)
    up, down = moves(True, lambda p: p + 1), moves(True, lambda p: p - 1)
    mate = pp(own, moves(False, near_mate))
    near = jnp.stack([own, mate])
    rest = pp(near, moves(False, far_mate))
    near_left = pp(near, up)
    near_right = pp(near, down)
    rest_right = pp(rest, down)
    rest_left = pp(rest, up)
    near_far = pp(near_left, up)
    rest_far = pp(rest_right, down)
    mine = [near, rest, near_right, rest_right, near_far, rest_far, near_left, rest_left]
    theirs = [pp(value, SWAP) for value in mine]
    return mine + theirs


def work(panels, reflectors, block_coeffs, block_mask, block_starts, carry_map):
    fronts = lax.axis_size("front")
    row = lax.axis_index("row").reshape(1)
    cols = panels.shape[2]
    part = cols // ROWS

    pieces = call(turn_kernel, shape((cols, SPAN)), [VMEM])(panels)
    own = call(
        mask_kernel,
        shape((SPAN, WIDTH)),
        [SMEM] + [HBM] * 3,
        limit=60,
        scratch=[
            pltpu.SMEM(block_mask.shape, I32),
            pltpu.SMEM(block_starts.shape, I32),
            pltpu.VMEM(reflectors.shape, BF),
            pltpu.SemaphoreType.DMA((3,)),
        ],
    )(row, block_mask, block_starts, reflectors)
    got = lax.all_to_all(pieces.reshape(ROWS, part, SPAN), "row", 0, 0, tiled=True)
    parts = gather_rows(own)

    order, spread = call(
        table_kernel, (shape((CARRIED, CARRIED)), shape((CARRIED, 8 * SPAN))), [VMEM]
    )(carry_map)

    eff, base, first, sent = call(
        base_kernel,
        (
            shape((ROWS, SPAN, WIDTH)),
            shape((part, WIDTH), F32),
            shape((part, CARRIED), F32),
            shape((part, CARRIED)),
        ),
        [SMEM] + [VMEM] * 18,
    )(row, *parts, got, block_coeffs)

    came = [lax.ppermute(sent, "front", [(0, 1)])]
    turn, hop = call(
        hop_kernel,
        (shape((CARRIED, WIDTH)), shape((CARRIED, CARRIED))),
        [VMEM] * 3,
        scratch=[pltpu.VMEM((WIDTH // 128, CARRIED, 128), F32), pltpu.VMEM((2, CARRIED, SPAN), F32)],
    )(carry_map, eff, block_coeffs)
    for step in range(2, fronts):
        sent = (first + mm(came[-1], hop)).astype(BF)
        came.append(lax.ppermute(sent, "front", [(step - 1, step)]))

    none = [jnp.zeros_like(sent)] * (7 - len(came))
    out = call(last_kernel, shape((ROWS, part, SPAN)), [VMEM] * 13)(
        *came, *none, base, turn, order, spread, got, eff
    )
    home = lax.all_to_all(out, "row", 0, 0, tiled=True)
    return home.reshape(cols, SPAN).T[None]


def solution(mesh):
    in_specs = (
        P("front", "row", None),
        P("front", "row", None),
        P("front", None, None),
        P("front", "row", None),
        P("front", None),
        P("front", None),
    )
    out_specs = P("front", "row", None)
    return jax.shard_map(work, mesh=mesh, in_specs=in_specs, out_specs=out_specs, check_vma=False)
```

```python
import jax
import jax.numpy as jnp
from jax import lax
from jax.experimental import pallas as pl
from jax.experimental.pallas import tpu as pltpu
from jax.sharding import PartitionSpec as P


BF = jnp.bfloat16
F32 = jnp.float32
I32 = jnp.int32
SIDE = 4
ROWS = 32
SPAN = 128
EACH = 32
CARRIED = ROWS * EACH
QUARTER = CARRIED // 4
TAIL = 24
WIDTH = 512


def mm(a, b, dims=((1,), (0,))):
    return lax.dot_general(a, b, (dims, ((), ())), preferred_element_type=F32)


def place(x, y, core):
    return ((x % SIDE) * SIDE + y % SIDE) * 2 + core


def moves(second, step):
    pairs = []
    for x in range(SIDE):
        for y in range(SIDE):
            for core in range(2):
                along_x = (core == 0) != second
                to_x, to_y = (step(x), y) if along_x else (x, step(y))
                pairs.append((place(x, y, core), place(to_x, to_y, core)))
    return pairs


def near_mate(p):
    return p ^ 1


def far_mate(p):
    return p + 1 if p % 2 else p - 1


SWAP = [(place(x, y, c), place(x, y, 1 - c)) for x in range(SIDE) for y in range(SIDE) for c in range(2)]

VMEM = pl.BlockSpec(memory_space=pltpu.VMEM)
HBM = pl.BlockSpec(memory_space=pltpu.HBM)


def call(kernel, outs, specs, limit=8, scratch=()):
    return pl.pallas_call(
        kernel,
        out_shape=outs,
        in_specs=specs,
        out_specs=jax.tree.map(lambda _: VMEM, outs),
        scratch_shapes=scratch,
        compiler_params=pltpu.CompilerParams(vmem_limit_bytes=limit << 20),
    )


def shape(dims, dtype=BF):
    return jax.ShapeDtypeStruct(dims, dtype)


def mask_kernel(mask, starts, refl, own, mask_s, starts_s, refl_v, sems):
    fetches = [
        pltpu.make_async_copy(source, target, sems.at[i])
        for i, (source, target) in enumerate(((refl, refl_v), (mask, mask_s), (starts, starts_s)))
    ]
    for fetch in fetches:
        fetch.start()
    for fetch in fetches:
        fetch.wait()
    ids = lax.axis_index("row") * SPAN + lax.broadcasted_iota(I32, (SPAN, 128), 0)
    for k in range(WIDTH // 128):
        kept = (ids >= starts_s[0, k]) & (mask_s[0, 0, k] == 1)
        part = refl_v[0, :, k * 128 : (k + 1) * 128].astype(F32)
        own[:, k * 128 : (k + 1) * 128] = jnp.where(kept, part, 0.0).astype(BF)


def turn_kernel(panels, out):
    for k in range(panels.shape[2] // 128):
        part = panels[0, :, k * 128 : (k + 1) * 128]
        out[k * 128 : (k + 1) * 128, :] = part.T


def slots(row, sibling):
    x, y, core = row // (2 * SIDE), (row // 2) % SIDE, row % 2
    who = 1 - core if sibling else core
    one, two = jnp.where(who == 0, x, y), jnp.where(who == 0, y, x)
    near = one + 1 - 2 * (one % 2)
    far = (one + SIDE - 1 + 2 * (one % 2)) % SIDE
    beyond = far + 1 - 2 * (far % 2)
    for j in range(SIDE):
        for k, held in enumerate((one, near, far, beyond)):
            other = (two + j) % SIDE
            at_x, at_y = jnp.where(who == 0, held, other), jnp.where(who == 0, other, held)
            yield j, k, (at_x * SIDE + at_y) * 2 + who


def product(row, mine, theirs, got, eff, acc):
    for sibling, parts in enumerate((mine, theirs)):
        held = None
        for j, k, block in slots(row, sibling):
            tile = parts[2 * j + k // 2][k % 2]
            if eff is not None:
                eff[block] = tile
            if held is None:
                held = (got[block], tile)
            else:
                lhs = jnp.concatenate([held[0], got[block]], axis=1)
                acc += mm(lhs, jnp.concatenate([held[1], tile], axis=0))
                held = None
    return acc


def first_kernel(*refs):
    mine, theirs, (got, coeffs, sent) = refs[:8], refs[8:16], refs[16:]

    front = lax.axis_index("front")

    @pl.when(front != 0)
    def _():
        sent[...] = jnp.zeros_like(sent)

    @pl.when(front == 0)
    def _():
        row = lax.axis_index("row")
        acc = product(row, mine, theirs, got, None, jnp.zeros((sent.shape[0], WIDTH), F32))
        m = mm(acc.astype(BF), coeffs[0]).astype(BF)
        for sibling, parts in enumerate((mine, theirs)):
            for j, k, block in slots(row, sibling):

                @pl.when(block >= TAIL)
                def _():
                    res = got[block].astype(F32) - mm(m, parts[2 * j + k // 2][k % 2], ((1,), (1,)))
                    sent[:, pl.ds(pl.multiple_of((block - TAIL) * SPAN, SPAN), SPAN)] = res.astype(BF)


def unfold(carry):
    rows = jnp.concatenate([carry[:, j * ROWS : (j + 1) * ROWS] for j in range(EACH)], axis=0)
    return rows - SPAN * lax.broadcasted_iota(I32, (EACH, ROWS), 1)


def base_kernel(*refs):
    mine, theirs, (got, coeffs, carry, eff, base, first, gath, wide) = refs[:8], refs[8:16], refs[16:]
    acc = product(lax.axis_index("row"), mine, theirs, got, eff, jnp.zeros(base.shape, F32))
    m = mm(acc.astype(BF), coeffs[0])
    base[...] = m
    m = m.astype(BF)
    for t in range(TAIL, ROWS, 2):
        low = eff[t : t + 2].reshape(2 * SPAN, WIDTH)
        have = jnp.concatenate([got[t], got[t + 1]], axis=1).astype(F32)
        first[:, (t - TAIL) * SPAN : (t - TAIL + 2) * SPAN] = have - mm(m, low, ((1,), (1,)))
    offsets = unfold(carry[...])
    lane = lax.broadcasted_iota(I32, (2 * EACH, 2 * SPAN), 1)
    for b in range(0, ROWS, 2):
        where = jnp.concatenate([offsets[:, b : b + 1], offsets[:, b + 1 : b + 2] + SPAN], axis=0)
        pick = (where == lane).astype(F32).astype(BF)
        rows = mm(pick, eff[b : b + 2].reshape(2 * SPAN, WIDTH))
        for h in range(2):
            for k in range(WIDTH // 128):
                tile = rows[h * EACH : (h + 1) * EACH, k * 128 : (k + 1) * 128]
                wide[k, pl.ds(b + h, EACH, stride=ROWS), :] = tile
    for k in range(WIDTH // 128):
        gath[:, k * 128 : (k + 1) * 128] = wide[k].astype(BF)


def second_kernel(came, first, gath, coeffs, eff, order, spread, sent):
    cin = came[...]
    w = mm(cin, gath[...]).astype(BF)
    t = mm(w, coeffs[0]).astype(BF)
    placed = mm(cin, order[:, CARRIED - QUARTER :]).astype(BF)
    moved = mm(placed, spread[CARRIED - QUARTER :, :])
    for b in range(TAIL, ROWS, 2):
        at = slice((b - TAIL) * SPAN, (b - TAIL + 2) * SPAN)
        down = mm(t, eff[b : b + 2].reshape(2 * SPAN, WIDTH), ((1,), (1,)))
        sent[:, at] = (first[:, at] + moved[:, at] - down).astype(BF)


def hop_kernel(carry, gath, eff, coeffs, turn, hop, fall):
    offsets = unfold(carry[...])
    for r in range(0, CARRIED, 256):
        turn[r : r + 256, :] = mm(gath[r : r + 256, :], coeffs[0]).astype(BF)
    lane = lax.broadcasted_iota(I32, (EACH, SPAN), 1)
    for t in range(TAIL, ROWS, 2):
        low = eff[t : t + 2].reshape(2 * SPAN, WIDTH)
        for r in range(0, CARRIED, 256):
            down = -mm(turn[r : r + 256, :], low, ((1,), (1,)))
            for h in range(2):
                fall[h, r : r + 256, :] = down[:, h * SPAN : (h + 1) * SPAN]
        for h in range(2):
            pick = (offsets[:, t + h : t + h + 1] == lane).astype(F32)
            at = (h, pl.ds(t + h, EACH, stride=ROWS), slice(None))
            fall[at] = fall[at] + pick
            hop[:, (t + h - TAIL) * SPAN : (t + h - TAIL + 1) * SPAN] = fall[h].astype(BF)


def table_kernel(carry, order, spread):
    offsets = unfold(carry[...])
    for r in range(0, CARRIED, 128):
        down = r + lax.broadcasted_iota(I32, (128, CARRIED), 0)
        right = lax.broadcasted_iota(I32, (128, CARRIED), 1)
        order[r : r + 128, :] = ((right % EACH) * ROWS + right // EACH == down).astype(F32).astype(BF)
    lane = lax.broadcasted_iota(I32, (EACH, 8 * SPAN), 1)
    for b in range(ROWS):
        where = offsets[:, b : b + 1] + (b % 8) * SPAN
        spread[b * EACH : (b + 1) * EACH, :] = (where == lane).astype(F32).astype(BF)


def last_kernel(c1, c2, c3, c4, c5, c6, c7, base, turn, order, spread, got, eff, out):
    cin = c1[...].astype(F32)
    for c in (c2, c3, c4, c5, c6, c7):
        cin += c[...].astype(F32)
    cin = cin.astype(BF)
    m = (base[...] + mm(cin, turn[...])).astype(BF)
    sorted_in = mm(cin, order[...]).astype(BF)
    for g in range(4):
        moved = mm(sorted_in[:, g * 256 : (g + 1) * 256], spread[g * 256 : (g + 1) * 256, :])
        for p in range(0, 8, 2):
            b = 8 * g + p
            have = jnp.concatenate([got[b], got[b + 1]], axis=1).astype(F32)
            a = (have + moved[:, p * SPAN : (p + 2) * SPAN]).astype(BF).astype(F32)
            back = mm(m, eff[b : b + 2].reshape(2 * SPAN, WIDTH), ((1,), (1,)))
            res = (a - back).astype(BF)
            out[b] = res[:, :SPAN]
            out[b + 1] = res[:, SPAN:]


def gather_rows(own):
    pp = lambda value, pairs: lax.ppermute(value, "row", pairs)
    up, down = moves(True, lambda p: p + 1), moves(True, lambda p: p - 1)
    mate = pp(own, moves(False, near_mate))
    near = jnp.stack([own, mate])
    rest = pp(near, moves(False, far_mate))
    near_left = pp(near, up)
    near_right = pp(near, down)
    rest_right = pp(rest, down)
    rest_left = pp(rest, up)
    near_far = pp(near_left, up)
    rest_far = pp(rest_right, down)
    mine = [near, rest, near_right, rest_right, near_far, rest_far, near_left, rest_left]
    theirs = [pp(value, SWAP) for value in mine]
    return mine + theirs


def work(panels, reflectors, block_coeffs, block_mask, block_starts, carry_map):
    fronts = lax.axis_size("front")
    cols = panels.shape[2]
    part = cols // ROWS

    pieces = call(turn_kernel, shape((cols, SPAN)), [VMEM])(panels)
    own = call(
        mask_kernel,
        shape((SPAN, WIDTH)),
        [HBM] * 3,
        limit=60,
        scratch=[
            pltpu.SMEM(block_mask.shape, I32),
            pltpu.SMEM(block_starts.shape, I32),
            pltpu.VMEM(reflectors.shape, BF),
            pltpu.SemaphoreType.DMA((3,)),
        ],
    )(block_mask, block_starts, reflectors)
    got = lax.all_to_all(pieces.reshape(ROWS, part, SPAN), "row", 0, 0, tiled=True)
    parts = gather_rows(own)
    order, spread = call(
        table_kernel, (shape((CARRIED, CARRIED)), shape((CARRIED, 8 * SPAN))), [VMEM]
    )(carry_map)

    sent = call(first_kernel, shape((part, CARRIED)), [VMEM] * 18)(*parts, got, block_coeffs)
    came = [lax.ppermute(sent, "front", [(0, 1)])]
    eff, base, first, gath = call(
        base_kernel,
        (
            shape((ROWS, SPAN, WIDTH)),
            shape((part, WIDTH), F32),
            shape((part, CARRIED), F32),
            shape((CARRIED, WIDTH)),
        ),
        [VMEM] * 19,
        scratch=[pltpu.VMEM((WIDTH // 128, CARRIED, 128), F32)],
    )(*parts, got, block_coeffs, carry_map)
    sent = call(second_kernel, shape((part, CARRIED)), [VMEM] * 7)(
        came[0], first, gath, block_coeffs, eff, order, spread
    )
    came.append(lax.ppermute(sent, "front", [(1, 2)]))
    turn, hop = call(
        hop_kernel,
        (shape((CARRIED, WIDTH)), shape((CARRIED, CARRIED))),
        [VMEM] * 4,
        scratch=[pltpu.VMEM((2, CARRIED, SPAN), F32)],
    )(carry_map, gath, eff, block_coeffs)
    for step in range(3, fronts):
        sent = (first + mm(came[-1], hop)).astype(BF)
        came.append(lax.ppermute(sent, "front", [(step - 1, step)]))

    out = call(last_kernel, shape((ROWS, part, SPAN)), [VMEM] * 13)(
        *came, *[jnp.zeros_like(sent)] * (7 - len(came)), base, turn, order, spread, got, eff
    )
    home = lax.all_to_all(out, "row", 0, 0, tiled=True)
    return home.reshape(cols, SPAN).T[None]


def solution(mesh):
    in_specs = (
        P("front", "row", None),
        P("front", "row", None),
        P("front", None, None),
        P("front", "row", None),
        P("front", None),
        P("front", None),
    )
    out_specs = P("front", "row", None)
    return jax.shard_map(work, mesh=mesh, in_specs=in_specs, out_specs=out_specs, check_vma=False)
```

```python
import jax
import jax.numpy as jnp
from jax import lax
from jax.experimental import pallas as pl
from jax.experimental.pallas import tpu as pltpu
from jax.sharding import PartitionSpec as P


BF = jnp.bfloat16
F32 = jnp.float32
I32 = jnp.int32
SIDE = 4
ROWS = 32
SPAN = 128
EACH = 32
CARRIED = ROWS * EACH
QUARTER = CARRIED // 4
TAIL = 24
WIDTH = 512


def mm(a, b, dims=((1,), (0,))):
    return lax.dot_general(a, b, (dims, ((), ())), preferred_element_type=F32)


def place(x, y, core):
    return ((x % SIDE) * SIDE + y % SIDE) * 2 + core


def moves(second, step):
    pairs = []
    for x in range(SIDE):
        for y in range(SIDE):
            for core in range(2):
                along_x = (core == 0) != second
                to_x, to_y = (step(x), y) if along_x else (x, step(y))
                pairs.append((place(x, y, core), place(to_x, to_y, core)))
    return pairs


SWAP = [(place(x, y, c), place(x, y, 1 - c)) for x in range(SIDE) for y in range(SIDE) for c in range(2)]

VMEM = pl.BlockSpec(memory_space=pltpu.VMEM)
HBM = pl.BlockSpec(memory_space=pltpu.HBM)


def call(kernel, outs, specs, limit=8, scratch=()):
    return pl.pallas_call(
        kernel,
        out_shape=outs,
        in_specs=specs,
        out_specs=jax.tree.map(lambda _: VMEM, outs),
        scratch_shapes=scratch,
        compiler_params=pltpu.CompilerParams(vmem_limit_bytes=limit << 20),
    )


def shape(dims, dtype=BF):
    return jax.ShapeDtypeStruct(dims, dtype)


def mask_kernel(mask, starts, refl, own, mask_s, starts_s, refl_v, sems):
    fetches = [
        pltpu.make_async_copy(source, target, sems.at[i])
        for i, (source, target) in enumerate(((refl, refl_v), (mask, mask_s), (starts, starts_s)))
    ]
    for fetch in fetches:
        fetch.start()
    for fetch in fetches:
        fetch.wait()
    ids = lax.axis_index("row") * SPAN + lax.broadcasted_iota(I32, (SPAN, 128), 0)
    for k in range(WIDTH // 128):
        kept = (ids >= starts_s[0, k]) & (mask_s[0, 0, k] == 1)
        part = refl_v[0, :, k * 128 : (k + 1) * 128].astype(F32)
        own[:, k * 128 : (k + 1) * 128] = jnp.where(kept, part, 0.0).astype(BF)


def turn_kernel(panels, out):
    for k in range(panels.shape[2] // 128):
        part = panels[0, :, k * 128 : (k + 1) * 128]
        out[k * 128 : (k + 1) * 128, :] = part.T


def slots(row, sibling):
    x, y, core = row // (2 * SIDE), (row // 2) % SIDE, row % 2
    who = 1 - core if sibling else core
    for j in range(SIDE):
        for k in range(SIDE):
            dx, dy = jnp.where(who == 0, k, j), jnp.where(who == 0, j, k)
            yield j, k, (((x + dx) % SIDE) * SIDE + (y + dy) % SIDE) * 2 + who


def product(row, mine, theirs, got, eff, acc):
    for sibling, parts in enumerate((mine, theirs)):
        held = None
        for j, k, block in slots(row, sibling):
            tile = parts[2 * j + k // 2][k % 2]
            if eff is not None:
                eff[block] = tile
            if held is None:
                held = (got[block], tile)
            else:
                lhs = jnp.concatenate([held[0], got[block]], axis=1)
                acc += mm(lhs, jnp.concatenate([held[1], tile], axis=0))
                held = None
    return acc


def first_kernel(*refs):
    mine, theirs, (got, coeffs, sent) = refs[:8], refs[8:16], refs[16:]

    front = lax.axis_index("front")

    @pl.when(front != 0)
    def _():
        sent[...] = jnp.zeros_like(sent)

    @pl.when(front == 0)
    def _():
        row = lax.axis_index("row")
        acc = product(row, mine, theirs, got, None, jnp.zeros((sent.shape[0], WIDTH), F32))
        m = mm(acc.astype(BF), coeffs[0]).astype(BF)
        for sibling, parts in enumerate((mine, theirs)):
            for j, k, block in slots(row, sibling):

                @pl.when(block >= TAIL)
                def _():
                    res = got[block].astype(F32) - mm(m, parts[2 * j + k // 2][k % 2], ((1,), (1,)))
                    sent[:, pl.ds(pl.multiple_of((block - TAIL) * SPAN, SPAN), SPAN)] = res.astype(BF)


def unfold(carry):
    rows = jnp.concatenate([carry[:, j * ROWS : (j + 1) * ROWS] for j in range(EACH)], axis=0)
    return rows - SPAN * lax.broadcasted_iota(I32, (EACH, ROWS), 1)


def base_kernel(*refs):
    mine, theirs, own = refs[:8], refs[8:16], refs[16:]
    got, coeffs, carry, eff, base, first, gath, order, spread, wide = own
    acc = product(lax.axis_index("row"), mine, theirs, got, eff, jnp.zeros(base.shape, F32))
    m = mm(acc.astype(BF), coeffs[0])
    base[...] = m
    m = m.astype(BF)
    for t in range(TAIL, ROWS, 2):
        low = eff[t : t + 2].reshape(2 * SPAN, WIDTH)
        have = jnp.concatenate([got[t], got[t + 1]], axis=1).astype(F32)
        first[:, (t - TAIL) * SPAN : (t - TAIL + 2) * SPAN] = have - mm(m, low, ((1,), (1,)))
    offsets = unfold(carry[...])
    lane = lax.broadcasted_iota(I32, (2 * EACH, 2 * SPAN), 1)
    for b in range(0, ROWS, 2):
        where = jnp.concatenate([offsets[:, b : b + 1], offsets[:, b + 1 : b + 2] + SPAN], axis=0)
        pick = (where == lane).astype(F32).astype(BF)
        rows = mm(pick, eff[b : b + 2].reshape(2 * SPAN, WIDTH))
        for h in range(2):
            for k in range(WIDTH // 128):
                tile = rows[h * EACH : (h + 1) * EACH, k * 128 : (k + 1) * 128]
                wide[k, pl.ds(b + h, EACH, stride=ROWS), :] = tile
    for k in range(WIDTH // 128):
        gath[:, k * 128 : (k + 1) * 128] = wide[k].astype(BF)
    fill_order(order, CARRIED - QUARTER)
    fill_spread(spread, offsets, TAIL)


def fill_order(order, start):
    for r in range(0, CARRIED, 128):
        down = r + lax.broadcasted_iota(I32, (128, order.shape[1]), 0)
        right = start + lax.broadcasted_iota(I32, (128, order.shape[1]), 1)
        order[r : r + 128, :] = ((right % EACH) * ROWS + right // EACH == down).astype(F32).astype(BF)


def fill_spread(spread, offsets, start):
    lane = lax.broadcasted_iota(I32, (EACH, 8 * SPAN), 1)
    for b in range(start, ROWS):
        where = offsets[:, b : b + 1] + (b % 8) * SPAN
        at = (b - start) * EACH
        spread[at : at + EACH, :] = (where == lane).astype(F32).astype(BF)


def second_kernel(came, first, gath, coeffs, eff, order, spread, sent):
    cin = came[...]
    w = mm(cin, gath[...]).astype(BF)
    t = mm(w, coeffs[0]).astype(BF)
    moved = mm(mm(cin, order[...]).astype(BF), spread[...])
    for b in range(TAIL, ROWS, 2):
        at = slice((b - TAIL) * SPAN, (b - TAIL + 2) * SPAN)
        down = mm(t, eff[b : b + 2].reshape(2 * SPAN, WIDTH), ((1,), (1,)))
        sent[:, at] = (first[:, at] + moved[:, at] - down).astype(BF)


def hop_kernel(carry, gath, eff, coeffs, turn, hop, fall):
    offsets = unfold(carry[...])
    for r in range(0, CARRIED, 256):
        turn[r : r + 256, :] = mm(gath[r : r + 256, :], coeffs[0]).astype(BF)
    lane = lax.broadcasted_iota(I32, (EACH, SPAN), 1)
    for t in range(TAIL, ROWS, 2):
        low = eff[t : t + 2].reshape(2 * SPAN, WIDTH)
        for r in range(0, CARRIED, 256):
            down = -mm(turn[r : r + 256, :], low, ((1,), (1,)))
            for h in range(2):
                fall[h, r : r + 256, :] = down[:, h * SPAN : (h + 1) * SPAN]
        for h in range(2):
            pick = (offsets[:, t + h : t + h + 1] == lane).astype(F32)
            at = (h, pl.ds(t + h, EACH, stride=ROWS), slice(None))
            fall[at] = fall[at] + pick
            hop[:, (t + h - TAIL) * SPAN : (t + h - TAIL + 1) * SPAN] = fall[h].astype(BF)


def table_kernel(carry, order, spread):
    fill_order(order, 0)
    fill_spread(spread, unfold(carry[...]), 0)


def last_kernel(c1, c2, c3, c4, c5, c6, c7, base, turn, order, spread, got, eff, out):
    cin = c1[...].astype(F32)
    for c in (c2, c3, c4, c5, c6, c7):
        cin += c[...].astype(F32)
    cin = cin.astype(BF)
    m = (base[...] + mm(cin, turn[...])).astype(BF)
    sorted_in = mm(cin, order[...]).astype(BF)
    for g in range(4):
        moved = mm(sorted_in[:, g * 256 : (g + 1) * 256], spread[g * 256 : (g + 1) * 256, :])
        for p in range(0, 8, 2):
            b = 8 * g + p
            have = jnp.concatenate([got[b], got[b + 1]], axis=1).astype(F32)
            a = (have + moved[:, p * SPAN : (p + 2) * SPAN]).astype(BF).astype(F32)
            back = mm(m, eff[b : b + 2].reshape(2 * SPAN, WIDTH), ((1,), (1,)))
            res = (a - back).astype(BF)
            out[b] = res[:, :SPAN]
            out[b + 1] = res[:, SPAN:]


def gather_rows(own):
    pp = lambda value, pairs: lax.ppermute(value, "row", pairs)
    half = own.shape[0] // 2
    along, back = moves(False, lambda p: p + 1), moves(False, lambda p: p - 1)
    up, down = moves(True, lambda p: p + 1), moves(True, lambda p: p - 1)
    right = pp(own, back)
    left = pp(own, along)
    far_a = pp(left[:half], along)
    far_b = pp(right[half:], back)
    near = jnp.stack([own, right])
    near_left = pp(near, up)
    near_right = pp(near, down)
    rest = jnp.stack([jnp.concatenate([far_a, far_b]), left])
    rest_right = pp(rest, down)
    rest_left = pp(rest, up)
    near_far = pp(near_left, up)
    rest_far = pp(rest_right, down)
    mine = [near, rest, near_right, rest_right, near_far, rest_far, near_left, rest_left]
    theirs = [pp(value, SWAP) for value in mine]
    return mine + theirs


def work(panels, reflectors, block_coeffs, block_mask, block_starts, carry_map):
    fronts = lax.axis_size("front")
    cols = panels.shape[2]
    part = cols // ROWS

    pieces = call(turn_kernel, shape((cols, SPAN)), [VMEM])(panels)
    own = call(
        mask_kernel,
        shape((SPAN, WIDTH)),
        [HBM] * 3,
        limit=60,
        scratch=[
            pltpu.SMEM(block_mask.shape, I32),
            pltpu.SMEM(block_starts.shape, I32),
            pltpu.VMEM(reflectors.shape, BF),
            pltpu.SemaphoreType.DMA((3,)),
        ],
    )(block_mask, block_starts, reflectors)
    got = lax.all_to_all(pieces.reshape(ROWS, part, SPAN), "row", 0, 0, tiled=True)
    parts = gather_rows(own)
    order, spread = call(
        table_kernel, (shape((CARRIED, CARRIED)), shape((CARRIED, 8 * SPAN))), [VMEM]
    )(carry_map)

    sent = call(first_kernel, shape((part, CARRIED)), [VMEM] * 18)(*parts, got, block_coeffs)
    came = [lax.ppermute(sent, "front", [(0, 1)])]
    eff, base, first, gath, low_order, low_spread = call(
        base_kernel,
        (
            shape((ROWS, SPAN, WIDTH)),
            shape((part, WIDTH), F32),
            shape((part, CARRIED), F32),
            shape((CARRIED, WIDTH)),
            shape((CARRIED, QUARTER)),
            shape((QUARTER, 8 * SPAN)),
        ),
        [VMEM] * 19,
        scratch=[pltpu.VMEM((WIDTH // 128, CARRIED, 128), F32)],
    )(*parts, got, block_coeffs, carry_map)
    sent = call(second_kernel, shape((part, CARRIED)), [VMEM] * 7)(
        came[0], first, gath, block_coeffs, eff, low_order, low_spread
    )
    came.append(lax.ppermute(sent, "front", [(1, 2)]))
    turn, hop = call(
        hop_kernel,
        (shape((CARRIED, WIDTH)), shape((CARRIED, CARRIED))),
        [VMEM] * 4,
        scratch=[pltpu.VMEM((2, CARRIED, SPAN), F32)],
    )(carry_map, gath, eff, block_coeffs)
    for step in range(3, fronts):
        sent = (first + mm(came[-1], hop)).astype(BF)
        came.append(lax.ppermute(sent, "front", [(step - 1, step)]))

    out = call(last_kernel, shape((ROWS, part, SPAN)), [VMEM] * 13)(
        *came, *[jnp.zeros_like(sent)] * (7 - len(came)), base, turn, order, spread, got, eff
    )
    home = lax.all_to_all(out, "row", 0, 0, tiled=True)
    return home.reshape(cols, SPAN).T[None]


def solution(mesh):
    in_specs = (
        P("front", "row", None),
        P("front", "row", None),
        P("front", None, None),
        P("front", "row", None),
        P("front", None),
        P("front", None),
    )
    out_specs = P("front", "row", None)
    return jax.shard_map(work, mesh=mesh, in_specs=in_specs, out_specs=out_specs, check_vma=False)
```

```python
import jax
import jax.numpy as jnp
from jax import lax
from jax.experimental import pallas as pl
from jax.experimental.pallas import tpu as pltpu
from jax.sharding import PartitionSpec as P


BF = jnp.bfloat16
F32 = jnp.float32
I32 = jnp.int32
SIDE = 4
ROWS = 32
SPAN = 128
EACH = 32
CARRIED = ROWS * EACH
QUARTER = CARRIED // 4
TAIL = 24
WIDTH = 512


def mm(a, b, dims=((1,), (0,))):
    return lax.dot_general(a, b, (dims, ((), ())), preferred_element_type=F32)


def place(x, y, core):
    return ((x % SIDE) * SIDE + y % SIDE) * 2 + core


def moves(second, step):
    pairs = []
    for x in range(SIDE):
        for y in range(SIDE):
            for core in range(2):
                along_x = (core == 0) != second
                to_x, to_y = (step(x), y) if along_x else (x, step(y))
                pairs.append((place(x, y, core), place(to_x, to_y, core)))
    return pairs


SWAP = [(place(x, y, c), place(x, y, 1 - c)) for x in range(SIDE) for y in range(SIDE) for c in range(2)]

VMEM = pl.BlockSpec(memory_space=pltpu.VMEM)
HBM = pl.BlockSpec(memory_space=pltpu.HBM)


def call(kernel, outs, specs, limit=8, scratch=()):
    return pl.pallas_call(
        kernel,
        out_shape=outs,
        in_specs=specs,
        out_specs=jax.tree.map(lambda _: VMEM, outs),
        scratch_shapes=scratch,
        compiler_params=pltpu.CompilerParams(vmem_limit_bytes=limit << 20),
    )


def shape(dims, dtype=BF):
    return jax.ShapeDtypeStruct(dims, dtype)


def entry_kernel(mask, starts, refl, panels, own, flip, mask_s, starts_s, refl_v, panels_v, sems):
    pairs = ((refl, refl_v), (mask, mask_s), (starts, starts_s), (panels, panels_v))
    fetches = [pltpu.make_async_copy(*pair, sems.at[i]) for i, pair in enumerate(pairs)]
    for fetch in fetches:
        fetch.start()
    for fetch in fetches[:3]:
        fetch.wait()
    ids = lax.axis_index("row") * SPAN + lax.broadcasted_iota(I32, (SPAN, 128), 0)
    for k in range(WIDTH // 128):
        kept = (ids >= starts_s[0, k]) & (mask_s[0, 0, k] == 1)
        part = refl_v[0, :, k * 128 : (k + 1) * 128].astype(F32)
        own[:, k * 128 : (k + 1) * 128] = jnp.where(kept, part, 0.0).astype(BF)
    fetches[3].wait()
    for k in range(panels_v.shape[2] // 128):
        flip[k * 128 : (k + 1) * 128, :] = panels_v[0, :, k * 128 : (k + 1) * 128].T


def slots(row, sibling):
    x, y, core = row // (2 * SIDE), (row // 2) % SIDE, row % 2
    who = 1 - core if sibling else core
    for j in range(SIDE):
        for k in range(SIDE):
            dx, dy = jnp.where(who == 0, k, j), jnp.where(who == 0, j, k)
            yield j, k, (((x + dx) % SIDE) * SIDE + (y + dy) % SIDE) * 2 + who


def product(row, mine, theirs, got, eff, acc):
    for sibling, parts in enumerate((mine, theirs)):
        held = None
        for j, k, block in slots(row, sibling):
            tile = parts[2 * j + k // 2][k % 2]
            if eff is not None:
                eff[block] = tile
            if held is None:
                held = (got[block], tile)
            else:
                lhs = jnp.concatenate([held[0], got[block]], axis=1)
                acc += mm(lhs, jnp.concatenate([held[1], tile], axis=0))
                held = None
    return acc


def first_kernel(*refs):
    mine, theirs, (got, coeffs, sent) = refs[:8], refs[8:16], refs[16:]

    front = lax.axis_index("front")

    @pl.when(front != 0)
    def _():
        sent[...] = jnp.zeros_like(sent)

    @pl.when(front == 0)
    def _():
        row = lax.axis_index("row")
        acc = product(row, mine, theirs, got, None, jnp.zeros((sent.shape[0], WIDTH), F32))
        m = mm(acc.astype(BF), coeffs[0]).astype(BF)
        for sibling, parts in enumerate((mine, theirs)):
            for j, k, block in slots(row, sibling):

                @pl.when(block >= TAIL)
                def _():
                    res = got[block].astype(F32) - mm(m, parts[2 * j + k // 2][k % 2], ((1,), (1,)))
                    sent[:, pl.ds(pl.multiple_of((block - TAIL) * SPAN, SPAN), SPAN)] = res.astype(BF)


def unfold(carry):
    rows = jnp.concatenate([carry[:, j * ROWS : (j + 1) * ROWS] for j in range(EACH)], axis=0)
    return rows - SPAN * lax.broadcasted_iota(I32, (EACH, ROWS), 1)


def base_kernel(*refs):
    mine, theirs, own = refs[:8], refs[8:16], refs[16:]
    got, coeffs, carry, eff, base, first, gath, order, spread, wide = own
    acc = product(lax.axis_index("row"), mine, theirs, got, eff, jnp.zeros(base.shape, F32))
    m = mm(acc.astype(BF), coeffs[0])
    base[...] = m
    m = m.astype(BF)
    for t in range(TAIL, ROWS, 2):
        low = eff[t : t + 2].reshape(2 * SPAN, WIDTH)
        have = jnp.concatenate([got[t], got[t + 1]], axis=1).astype(F32)
        first[:, (t - TAIL) * SPAN : (t - TAIL + 2) * SPAN] = have - mm(m, low, ((1,), (1,)))
    offsets = unfold(carry[...])
    lane = lax.broadcasted_iota(I32, (2 * EACH, 2 * SPAN), 1)
    for b in range(0, ROWS, 2):
        where = jnp.concatenate([offsets[:, b : b + 1], offsets[:, b + 1 : b + 2] + SPAN], axis=0)
        pick = (where == lane).astype(F32).astype(BF)
        rows = mm(pick, eff[b : b + 2].reshape(2 * SPAN, WIDTH))
        for h in range(2):
            for k in range(WIDTH // 128):
                tile = rows[h * EACH : (h + 1) * EACH, k * 128 : (k + 1) * 128]
                wide[k, pl.ds(b + h, EACH, stride=ROWS), :] = tile
    for k in range(WIDTH // 128):
        gath[:, k * 128 : (k + 1) * 128] = wide[k].astype(BF)
    fill_order(order, CARRIED - QUARTER)
    fill_spread(spread, offsets, TAIL)


def fill_order(order, start):
    for r in range(0, CARRIED, 128):
        down = r + lax.broadcasted_iota(I32, (128, order.shape[1]), 0)
        right = start + lax.broadcasted_iota(I32, (128, order.shape[1]), 1)
        order[r : r + 128, :] = ((right % EACH) * ROWS + right // EACH == down).astype(F32).astype(BF)


def fill_spread(spread, offsets, start):
    lane = lax.broadcasted_iota(I32, (EACH, 8 * SPAN), 1)
    for b in range(start, ROWS):
        where = offsets[:, b : b + 1] + (b % 8) * SPAN
        at = (b - start) * EACH
        spread[at : at + EACH, :] = (where == lane).astype(F32).astype(BF)


def second_kernel(came, first, gath, coeffs, eff, order, spread, sent):
    cin = came[...]
    w = mm(cin, gath[...]).astype(BF)
    t = mm(w, coeffs[0]).astype(BF)
    moved = mm(mm(cin, order[...]).astype(BF), spread[...])
    for b in range(TAIL, ROWS, 2):
        at = slice((b - TAIL) * SPAN, (b - TAIL + 2) * SPAN)
        down = mm(t, eff[b : b + 2].reshape(2 * SPAN, WIDTH), ((1,), (1,)))
        sent[:, at] = (first[:, at] + moved[:, at] - down).astype(BF)


def hop_kernel(carry, gath, eff, coeffs, turn, hop, fall):
    offsets = unfold(carry[...])
    for r in range(0, CARRIED, 256):
        turn[r : r + 256, :] = mm(gath[r : r + 256, :], coeffs[0]).astype(BF)
    lane = lax.broadcasted_iota(I32, (EACH, SPAN), 1)
    for t in range(TAIL, ROWS, 2):
        low = eff[t : t + 2].reshape(2 * SPAN, WIDTH)
        for r in range(0, CARRIED, 256):
            down = -mm(turn[r : r + 256, :], low, ((1,), (1,)))
            for h in range(2):
                fall[h, r : r + 256, :] = down[:, h * SPAN : (h + 1) * SPAN]
        for h in range(2):
            pick = (offsets[:, t + h : t + h + 1] == lane).astype(F32)
            at = (h, pl.ds(t + h, EACH, stride=ROWS), slice(None))
            fall[at] = fall[at] + pick
            hop[:, (t + h - TAIL) * SPAN : (t + h - TAIL + 1) * SPAN] = fall[h].astype(BF)


def table_kernel(carry, order, spread):
    fill_order(order, 0)
    fill_spread(spread, unfold(carry[...]), 0)


def last_kernel(c1, c2, c3, c4, c5, c6, c7, base, turn, order, spread, got, eff, out):
    cin = c1[...].astype(F32)
    for c in (c2, c3, c4, c5, c6, c7):
        cin += c[...].astype(F32)
    cin = cin.astype(BF)
    m = (base[...] + mm(cin, turn[...])).astype(BF)
    sorted_in = mm(cin, order[...]).astype(BF)
    for g in range(4):
        moved = mm(sorted_in[:, g * 256 : (g + 1) * 256], spread[g * 256 : (g + 1) * 256, :])
        for p in range(0, 8, 2):
            b = 8 * g + p
            have = jnp.concatenate([got[b], got[b + 1]], axis=1).astype(F32)
            a = (have + moved[:, p * SPAN : (p + 2) * SPAN]).astype(BF).astype(F32)
            back = mm(m, eff[b : b + 2].reshape(2 * SPAN, WIDTH), ((1,), (1,)))
            res = (a - back).astype(BF)
            out[b] = res[:, :SPAN]
            out[b + 1] = res[:, SPAN:]


def gather_rows(own):
    pp = lambda value, pairs: lax.ppermute(value, "row", pairs)
    half = own.shape[0] // 2
    along, back = moves(False, lambda p: p + 1), moves(False, lambda p: p - 1)
    up, down = moves(True, lambda p: p + 1), moves(True, lambda p: p - 1)
    right = pp(own, back)
    left = pp(own, along)
    far_a = pp(left[:half], along)
    far_b = pp(right[half:], back)
    near = jnp.stack([own, right])
    near_left = pp(near, up)
    near_right = pp(near, down)
    rest = jnp.stack([jnp.concatenate([far_a, far_b]), left])
    rest_right = pp(rest, down)
    rest_left = pp(rest, up)
    near_far = pp(near_left, up)
    rest_far = pp(rest_right, down)
    mine = [near, rest, near_right, rest_right, near_far, rest_far, near_left, rest_left]
    theirs = [pp(value, SWAP) for value in mine]
    return mine + theirs


def work(panels, reflectors, block_coeffs, block_mask, block_starts, carry_map):
    fronts = lax.axis_size("front")
    cols = panels.shape[2]
    part = cols // ROWS

    own, pieces = call(
        entry_kernel,
        (shape((SPAN, WIDTH)), shape((cols, SPAN))),
        [HBM] * 4,
        limit=60,
        scratch=[
            pltpu.SMEM(block_mask.shape, I32),
            pltpu.SMEM(block_starts.shape, I32),
            pltpu.VMEM(reflectors.shape, BF),
            pltpu.VMEM(panels.shape, BF),
            pltpu.SemaphoreType.DMA((4,)),
        ],
    )(block_mask, block_starts, reflectors, panels)
    got = lax.all_to_all(pieces.reshape(ROWS, part, SPAN), "row", 0, 0, tiled=True)
    parts = gather_rows(own)
    order, spread = call(
        table_kernel, (shape((CARRIED, CARRIED)), shape((CARRIED, 8 * SPAN))), [VMEM]
    )(carry_map)

    sent = call(first_kernel, shape((part, CARRIED)), [VMEM] * 18)(*parts, got, block_coeffs)
    came = [lax.ppermute(sent, "front", [(0, 1)])]
    eff, base, first, gath, low_order, low_spread = call(
        base_kernel,
        (
            shape((ROWS, SPAN, WIDTH)),
            shape((part, WIDTH), F32),
            shape((part, CARRIED), F32),
            shape((CARRIED, WIDTH)),
            shape((CARRIED, QUARTER)),
            shape((QUARTER, 8 * SPAN)),
        ),
        [VMEM] * 19,
        scratch=[pltpu.VMEM((WIDTH // 128, CARRIED, 128), F32)],
    )(*parts, got, block_coeffs, carry_map)
    sent = call(second_kernel, shape((part, CARRIED)), [VMEM] * 7)(
        came[0], first, gath, block_coeffs, eff, low_order, low_spread
    )
    came.append(lax.ppermute(sent, "front", [(1, 2)]))
    turn, hop = call(
        hop_kernel,
        (shape((CARRIED, WIDTH)), shape((CARRIED, CARRIED))),
        [VMEM] * 4,
        scratch=[pltpu.VMEM((2, CARRIED, SPAN), F32)],
    )(carry_map, gath, eff, block_coeffs)
    for step in range(3, fronts):
        sent = (first + mm(came[-1], hop)).astype(BF)
        came.append(lax.ppermute(sent, "front", [(step - 1, step)]))

    out = call(last_kernel, shape((ROWS, part, SPAN)), [VMEM] * 13)(
        *came, *[jnp.zeros_like(sent)] * (7 - len(came)), base, turn, order, spread, got, eff
    )
    home = lax.all_to_all(out, "row", 0, 0, tiled=True)
    return home.reshape(cols, SPAN).T[None]


def solution(mesh):
    in_specs = (
        P("front", "row", None),
        P("front", "row", None),
        P("front", None, None),
        P("front", "row", None),
        P("front", None),
        P("front", None),
    )
    out_specs = P("front", "row", None)
    return jax.shard_map(work, mesh=mesh, in_specs=in_specs, out_specs=out_specs, check_vma=False)
```
